32 devices in a mesh: group: 4 (over z), shard: 8 (over y, x, core).
Axes of the slice: x: 2, y: 2, z: 4, core: 2. Of those that a mesh axis runs over, the one named last changes fastest.
Arguments:
- tokens: bfloat16 [49152, 1024], P(('group', 'shard')), may hold values from -36 to 36
- cotangent: bfloat16 [49152, 1024], P(('group', 'shard')), may hold values from -0.43164062 to 0.43164062
- master: float32 [4096, 4096], P(('group', 'shard')), may hold values from -0.03125 to 0.03125
- moment_one: float32 [4096, 4096], P(('group', 'shard')), may hold values from -2 to 2
- moment_two: float32 [4096, 4096], P(('group', 'shard')), may hold values from 0.05 to 2
- anchor: float32 [1024, 4096], P('shard'), may hold values from -0.03125 to 0.03125
- outer_momentum: float32 [1024, 4096], P('shard'), may hold values from -0.02 to 0.02
Outputs:
- moment_one_next: float32 [4096, 4096], P(('group', 'shard'))
- moment_two_next: float32 [4096, 4096], P(('group', 'shard'))
- momentum_next: float32 [1024, 4096], P('shard')
- anchor_next: float32 [1024, 4096], P('shard')
The draws below stay inside these ranges and needn't reach their ends.
All inputs are finite; a program needn't handle non-finite values.
Results may differ from the reference program's by a relative error of at most 0.0047.
Values may be sent and summed in bfloat16 or wider, within the bound.
No kernel may reach another device: no remote copies, remote signals or barrier semaphores. Data moves between devices by JAX's collectives and lax.ppermute only.
A program may use at most 128 MiB of HBM per device.

```python
import math
import jax
import jax.numpy as jnp
from jax import lax

D = 1024
FF = 2048
TOK_DEV = 1536
TOKENS = 49152
ROWS = 4096
N_GROUP = 4
N_SHARD = 8


def steps_of(stream_key, shape, split, smallest, high):
    factor_of, own = 1.0, jax.random.fold_in(stream_key, 6)
    for position, blocks in split:
        steps = jnp.exp(jax.random.uniform(jax.random.fold_in(own, position), (blocks,), jnp.float32, smallest / len(split), high / len(split)))
        factor_of = factor_of * jnp.repeat(steps, shape[position] // blocks).reshape([-1 if axis == position else 1 for axis in range(len(shape))])
    return factor_of


def gaussian(key, dims, spread, limit, shards=(), kind=jnp.bfloat16):
    gain = steps_of(key, dims, shards, -0.22, 0.18) if shards else 1.0
    entries = jax.random.normal(key, dims, jnp.float32) * spread * gain
    return jnp.minimum(jnp.maximum(entries, -limit), limit).astype(kind)


def setup_inputs(seed: int = 0) -> dict:
    seeds = jax.random.split(jax.random.key(seed), 8)
    return {
        "tokens": gaussian(seeds[0], (TOKENS, D), 6.0, 36.0, ((0, 32),)),
        "cotangent": gaussian(seeds[1], (TOKENS, D), (8.0 / (TOK_DEV * N_SHARD) ** 0.5), 0.43164062, ((0, 32),)),
        "master": gaussian(seeds[2], (ROWS, 2 * FF), (36 * D) ** -0.5, 0.03125, ((0, 32),), jnp.float32),
        "moment_one": gaussian(seeds[3], (ROWS, 2 * FF), 0.3, 2.0, ((0, 32),), jnp.float32),
        "moment_two": jnp.clip(jnp.exp(math.log(2.0) - 3.6888794 * jax.random.uniform(seeds[4], (ROWS, 2 * FF), jnp.float32) ** steps_of(seeds[4], (ROWS, 2 * FF), ((0, 32),), -0.2, 0.2)), 0.05, 2.0),
        "anchor": gaussian(seeds[5], (D, 2 * FF), (36 * D) ** -0.5, 0.03125, ((0, 8),), jnp.float32),
        "outer_momentum": gaussian(seeds[6], (D, 2 * FF), 0.0033, 0.02, ((0, 8),), jnp.float32),
    }


first_correction = 0.9999734386011124
second_correction = 0.994079470779664

def gelu_tanh(values):
    return jax.nn.gelu(values, approximate=True)

def reference(tokens, cotangent, master, moment_one, moment_two, anchor, outer_momentum):
    group_rows = TOK_DEV * N_SHARD
    total = jnp.zeros(anchor.shape, jnp.float32)
    first_list = []
    second_list = []
    for group in range(N_GROUP):
        inputs = tokens[group * group_rows:(group + 1) * group_rows]
        upstream = cotangent[group * group_rows:(group + 1) * group_rows]
        params = master[group * D:(group + 1) * D]
        working = params.astype(jnp.bfloat16)
        pre = jnp.dot(inputs, working[:, :FF], preferred_element_type=jnp.float32)
        back = jnp.dot(upstream, working[:, FF:], preferred_element_type=jnp.float32)
        act = gelu_tanh(pre).astype(jnp.bfloat16)
        _, pullback = jax.vjp(gelu_tanh, pre)
        dpre = pullback(back)[0].astype(jnp.bfloat16)
        grad_in = lax.dot_general(inputs, dpre, (((0,), (0,)), ((), ())), preferred_element_type=jnp.float32)
        grad_out = lax.dot_general(upstream, act, (((0,), (0,)), ((), ())), preferred_element_type=jnp.float32)
        grad = jnp.concatenate([grad_in, grad_out], axis=1)
        first = 0.9 * moment_one[group * D:(group + 1) * D] + 0.1 * grad
        second = 0.95 * moment_two[group * D:(group + 1) * D] + 0.05 * grad * grad
        update = first / first_correction / (jnp.sqrt(second / second_correction) + 1e-08)
        inner = params - 0.001 * (update + 0.1 * params)
        total = total + (anchor - inner)
        first_list.append(first)
        second_list.append(second)
    mean_delta = total / N_GROUP
    momentum_next = 0.9 * outer_momentum + mean_delta
    anchor_next = anchor - 0.7 * (mean_delta + 0.9 * momentum_next)
    return (jnp.concatenate(first_list, axis=0), jnp.concatenate(second_list, axis=0), momentum_next, anchor_next)
```

```python
import functools

import jax
import jax.numpy as jnp
from jax import lax
from jax.experimental import pallas as pl
from jax.experimental.pallas import tpu as pltpu
from jax.sharding import PartitionSpec as P


first_correction = 0.9999734386011124
second_correction = 0.994079470779664

CHUNKS = 4
GATHERS = ((0,), (1,), (2, 3))
TOKEN_BLOCK = 512
f32, bf16 = jnp.float32, jnp.bfloat16


def bits_of(count):
    return [1 << k for k in range(count.bit_length() - 1)]


def chip_orders(shard_count):
    bits = bits_of(shard_count // 2)
    return bits, bits[1:] + bits[:1]


def chip_permutation(shard_count, step):
    orders = chip_orders(shard_count)
    return [(i, i ^ (2 * orders[i % 2][step])) for i in range(shard_count)]


def core_exchange(array):
    count = lax.axis_size("shard")
    return lax.ppermute(array, "shard", [(i, i ^ 1) for i in range(count)])


def chip_masks(shard_count, core):
    orders = chip_orders(shard_count)
    masks = []
    for key in range(shard_count // 2):
        pair = [0, 0]
        for step in range(len(orders[0])):
            if key >> step & 1:
                pair = [pair[0] ^ orders[0][step], pair[1] ^ orders[1][step]]
        masks.append(jnp.where(core == 0, pair[0], pair[1]))
    return masks


def vmem(limit):
    return pltpu.CompilerParams(vmem_limit_bytes=limit << 20)


VMEM = pl.BlockSpec(memory_space=pltpu.VMEM)
SMEM = pl.BlockSpec(memory_space=pltpu.SMEM)
ANY = pl.BlockSpec(memory_space=pl.ANY)


def split_kernel(half, starts, place_ref, master_ref, *out_refs):
    core = place_ref[0]
    width = master_ref.shape[1] // 2
    for a, start in enumerate(starts):
        for s in range(2):
            out = out_refs[2 * a + s]
            for io in range(2):
                at = pl.multiple_of(io * width + (core ^ s) * half + start, 128)
                out[io] = master_ref[:, pl.ds(at, out.shape[2])].astype(bf16)


def split_master(master, place, half, starts, spans):
    rows, _ = master.shape
    shapes = [jax.ShapeDtypeStruct((2, rows, span), bf16) for span in spans for _ in range(2)]
    outs = pl.pallas_call(
        functools.partial(split_kernel, half, starts),
        out_shape=shapes,
        in_specs=[SMEM, VMEM],
        out_specs=[VMEM] * len(shapes),
        compiler_params=vmem(4),
        name="split_master",
    )(place, master)
    return outs[0::2], outs[1::2]


def grad_kernel(pieces, start, place_ref, *refs):
    piece_refs = refs[:pieces]
    own_t, other_t, own_c, other_c = refs[pieces : pieces + 4]
    keep_ref, send_ref, w_in, w_out, acc_in, acc_out = refs[pieces + 4 :]
    core = place_ref[0]
    rows = piece_refs[0].shape[2]
    chunk = w_in.shape[1]

    def offset(key, s):
        return pl.multiple_of((place_ref[1 + key] * 2 + (core ^ s)) * rows, rows)

    for key, ref in enumerate(piece_refs):
        for s in range(2):
            w_in[pl.ds(offset(key, s), rows), :] = ref[s, 0, :, start : start + chunk]
            w_out[pl.ds(offset(key, s), rows), :] = ref[s, 1, :, start : start + chunk]

    c0 = 0.7978845608028654
    c1 = c0 * 0.044715
    dims = (((0,), (0,)), ((), ()))
    block = min(TOKEN_BLOCK, own_t.shape[0])
    pending = None
    filled = False

    def accumulate(dpre, act, inputs, upstream):
        if filled:
            acc_in[...] += lax.dot_general(inputs, dpre, dims, preferred_element_type=f32)
            acc_out[...] += lax.dot_general(upstream, act, dims, preferred_element_type=f32)
        else:
            acc_in[...] = lax.dot_general(inputs, dpre, dims, preferred_element_type=f32)
            acc_out[...] = lax.dot_general(upstream, act, dims, preferred_element_type=f32)

    for t_ref, c_ref in ((own_t, own_c), (other_t, other_c)):
        for k in range(own_t.shape[0] // block):
            inputs, upstream = t_ref[k * block : (k + 1) * block], c_ref[k * block : (k + 1) * block]
            pre = jnp.dot(inputs, w_in[...], preferred_element_type=f32)
            back = jnp.dot(upstream, w_out[...], preferred_element_type=f32)
            if pending is not None:
                accumulate(*pending)
                filled = True
            square = pre * pre
            t = jnp.tanh(pre * (c0 + c1 * square))
            gate = 0.5 + 0.5 * t
            act = (pre * gate).astype(bf16)
            slope = gate + (0.5 * pre) * (1.0 - t * t) * (c0 + (3.0 * c1) * square)
            pending = ((back * slope).astype(bf16), act, inputs, upstream)
    accumulate(*pending)
    for io, acc in enumerate((acc_in, acc_out)):
        for key in range(pieces):
            for s in range(2):
                term = acc[pl.ds(offset(key, s), rows), :]
                if key % 2:
                    send_ref[key // 2, s, io] = term.astype(bf16)
                else:
                    keep_ref[key // 2, s, io] = term


def gradient_terms(weights, start, chunk, tokens, tokens_other, cotangent, cotangent_other, place):
    pieces = len(weights)
    rows = weights[0].shape[2]
    depth = tokens.shape[1]
    out = (pieces // 2, 2, 2, rows, chunk)
    flops = 8 * 2 * tokens.shape[0] * depth * chunk
    return pl.pallas_call(
        functools.partial(grad_kernel, pieces, start),
        out_shape=[jax.ShapeDtypeStruct(out, f32), jax.ShapeDtypeStruct(out, bf16)],
        in_specs=[SMEM] + [VMEM] * (pieces + 4),
        out_specs=[VMEM] * 2,
        scratch_shapes=[
            pltpu.VMEM((depth, chunk), bf16),
            pltpu.VMEM((depth, chunk), bf16),
            pltpu.VMEM((depth, chunk), f32),
            pltpu.VMEM((depth, chunk), f32),
        ],
        cost_estimate=pl.CostEstimate(
            flops=flops, bytes_accessed=8 * tokens.size, transcendentals=2 * tokens.shape[0] * chunk
        ),
        compiler_params=vmem(20),
        name="gradient_terms",
    )(place, *weights, tokens, tokens_other, cotangent, cotangent_other)


def inner_kernel(start, place_ref, own_ref, other_ref, one_ref, two_ref, master_ref, anchor_ref, *refs):
    first_ref, second_ref, delta_ref = refs[-3:]
    window = pl.program_id(0)
    chunk = first_ref.shape[1]
    half = master_ref.shape[1] // 4
    io = window // 2
    mine = window % 2 == place_ref[0]
    at = pl.ds(pl.multiple_of(window * half + start, 128), chunk)
    grad = jnp.where(mine, own_ref[io], other_ref[io])
    master = master_ref[:, at]
    first = 0.9 * one_ref[:, at] + 0.1 * grad
    second = 0.95 * two_ref[:, at] + 0.05 * grad * grad
    update = first / first_correction / (jnp.sqrt(second / second_correction) + 1e-08)
    inner = master - 0.001 * (update + 0.1 * master)
    first_ref[...] = first
    second_ref[...] = second
    delta_ref[window] = (anchor_ref[:, at] - inner).astype(bf16)


def inner_step(own, other, start, chunk, moment_one, moment_two, master, anchor, place, held):
    rows, columns = master.shape
    half = columns // 4
    wide = pl.BlockSpec((rows, chunk), lambda i: (0, i * (half // chunk) + start // chunk))
    whole = jax.ShapeDtypeStruct((rows, columns), f32)
    held = () if held is None else held
    return pl.pallas_call(
        functools.partial(inner_kernel, start),
        out_shape=[whole, whole, jax.ShapeDtypeStruct((4, rows, chunk), bf16)],
        grid=(4,),
        in_specs=[SMEM] + [VMEM] * 6 + [ANY] * len(held),
        out_specs=[wide, wide, VMEM],
        input_output_aliases={7 + k: k for k in range(len(held))},
        cost_estimate=pl.CostEstimate(
            flops=80 * rows * chunk, bytes_accessed=4 * 4 * 2 * rows * chunk, transcendentals=8 * rows * chunk
        ),
        compiler_params=vmem(4),
        name="inner_step",
    )(place, own, other, moment_one, moment_two, master, anchor, *held)


def outer_kernel(groups, start, sum_ref, last_ref, anchor_ref, momentum_ref, *refs):
    momentum_out, anchor_out = refs[-2:]
    window = pl.program_id(0)
    chunk = momentum_out.shape[1]
    half = anchor_ref.shape[1] // 4
    at = pl.ds(pl.multiple_of(window * half + start, 128), chunk)
    mean_delta = (sum_ref[window].astype(f32) + last_ref[window].astype(f32)) / groups
    momentum_next = 0.9 * momentum_ref[:, at] + mean_delta
    momentum_out[...] = momentum_next
    anchor_out[...] = anchor_ref[:, at] - 0.7 * (mean_delta + 0.9 * momentum_next)


def outer_step(total, last, start, chunk, anchor, momentum, held):
    rows, columns = anchor.shape
    half = columns // 4
    wide = pl.BlockSpec((rows, chunk), lambda i: (0, i * (half // chunk) + start // chunk))
    whole = jax.ShapeDtypeStruct((rows, columns), f32)
    held = () if held is None else held
    return pl.pallas_call(
        functools.partial(outer_kernel, lax.axis_size("group"), start),
        out_shape=[whole, whole],
        grid=(4,),
        in_specs=[VMEM] * 4 + [ANY] * len(held),
        out_specs=[wide, wide],
        input_output_aliases={4 + k: k for k in range(len(held))},
        cost_estimate=pl.CostEstimate(flops=40 * rows * chunk, bytes_accessed=4 * 8 * rows * chunk, transcendentals=0),
        compiler_params=vmem(4),
        name="outer_step",
    )(total, last, anchor, momentum, *held)


def body(tokens, cotangent, master, moment_one, moment_two, anchor, outer_momentum):
    count = lax.axis_size("shard")
    groups = lax.axis_size("group")
    me = lax.axis_index("shard")
    core, chip = me % 2, me // 2
    place = jnp.stack([core] + [chip ^ mask for mask in chip_masks(count, core)]).astype(jnp.int32)
    half = master.shape[1] // 4
    chunk = half // CHUNKS
    levels = len(bits_of(count // 2))
    starts = [group[0] * chunk for group in GATHERS]
    spans = [len(group) * chunk for group in GATHERS]

    own, other = split_master(master, place, half, starts, spans)
    weights = {}
    for a, group in enumerate(GATHERS):
        received = core_exchange(other[a])
        pieces = {0: jnp.stack([own[a], received])}
        for step in range(levels):
            permutation = chip_permutation(count, step)
            for key in list(pieces):
                pieces[key | 1 << step] = lax.ppermute(pieces[key], "shard", permutation)
        for index in group:
            weights[index] = [pieces[key] for key in range(count // 2)], (index - group[0]) * chunk
    tokens_other = core_exchange(tokens)
    cotangent_other = core_exchange(cotangent)

    moments = outer = None
    for index in range(CHUNKS):
        keep, send = gradient_terms(
            *weights[index], chunk, tokens, tokens_other, cotangent, cotangent_other, place
        )
        blocks = keep
        for step in range(levels):
            received = lax.ppermute(send, "shard", chip_permutation(count, step))
            blocks = blocks + received.astype(f32)
            if step + 1 < levels:
                send = blocks[1::2].astype(bf16)
                blocks = blocks[0::2]
        grad_other = core_exchange(blocks[0, 1])
        first, second, delta = inner_step(
            blocks[0, 0], grad_other, index * chunk, chunk, moment_one, moment_two, master, anchor, place, moments
        )
        moments = (first, second)
        total = delta
        group_bits = bits_of(groups)
        for bit in group_bits:
            last = lax.ppermute(total, "group", [(i, i ^ bit) for i in range(groups)])
            if bit != group_bits[-1]:
                total = (total.astype(f32) + last.astype(f32)).astype(bf16)
        outer = outer_step(total, last, index * chunk, chunk, anchor, outer_momentum, outer)
    return (*moments, *outer)


def solution(mesh):
    placed = (
        P(("group", "shard"), None),
        P(("group", "shard"), None),
        P(("group", "shard"), None),
        P(("group", "shard"), None),
        P(("group", "shard"), None),
        P("shard", None),
        P("shard", None),
    )
    return jax.shard_map(
        body,
        mesh=mesh,
        in_specs=placed,
        out_specs=(
            P(("group", "shard"), None),
            P(("group", "shard"), None),
            P("shard", None),
            P("shard", None),
        ),
        check_vma=False,
    )
```
